128 devices in a mesh: pair: 16 (over z, x), aux: 8 (over y, core).
Axes of the slice: x: 4, y: 4, z: 4, core: 2. Of those that a mesh axis runs over, the one named last changes fastest.
Arguments:
- integrals: bfloat16 [3072, 8192], P(('aux', 'pair')), may hold values from -0.796875 to 0.796875
- metric: bfloat16 [3072, 3072], P('aux'), may hold values from -0.109375 to 0.109375
- occ_energy: float32 [8], replicated, may hold values from -1.5 to -0.3
- virt_energy: float32 [1024], replicated, may hold values from 0.3 to 3
- pair_table: int32 [32, 2], P('pair'), may hold values from 0 to 7, as said below
- pair_count: int32 [16], P('pair'), may hold values from 1 to 2, as said below
Outputs:
- grad_blocks: float32 [3072, 8192], P('aux', 'pair')
The draws below stay inside these ranges and needn't reach their ends.
Inputs may be any that keep to these rules, and one draw needn't show every extreme that they name: `pair_table`: occupied indices of the batch; slots beyond an owner's count hold valid but unused indices. `pair_count`: some owner holds exactly 2 listed pairs.
All inputs are finite; a program needn't handle non-finite values.
Results may differ from the reference program's by a relative error of at most 0.0028.
Values may be sent and summed in bfloat16 or wider, within the bound.
A program may use at most 128 MiB of HBM per device.

```python
import jax
import jax.numpy as jnp
from jax import lax

NAUX = 3072
NVIRT = 1024
OCC = 8
CAP = 2
OWNERS = 16
SLOTS = 32
N_AUX = 8


def draw_pair_count(key, part):
    first_key, second_key = jax.random.split(jax.random.fold_in(key, 11))
    counts = jax.random.randint(first_key, (OWNERS,), 1, CAP + 1)
    busiest = jax.random.randint(second_key, (), 0, OWNERS)
    return jnp.where(jnp.arange(OWNERS) == busiest, CAP, counts).astype(jnp.int32)


def draw_pair_table(key, part):
    return jax.random.randint(jax.random.fold_in(key, 23), (SLOTS, 2), 0, OCC).astype(jnp.int32)


def block_scale(stream_key, extent, shards, low, largest):
    def one(axis_at, shards_of):
        steps = jax.random.uniform(jax.random.fold_in(jax.random.fold_in(stream_key, 6), axis_at), (shards_of,), jnp.float32, low / len(shards), largest / len(shards))
        return jnp.repeat(jnp.exp(steps), extent[axis_at] // shards_of).reshape((-1,) + (1,) * (len(extent) - axis_at - 1))

    level = one(*shards[0])
    for cut in shards[1:]:
        level = level * one(*cut)
    return level


def scatter_about(stream_key, shape, deviation, bound, cuts=(), kind=jnp.bfloat16):
    entries = jax.random.normal(stream_key, shape, jnp.float32) * deviation
    if len(cuts) > 0:
        entries = block_scale(stream_key, shape, cuts, -0.22, 0.18) * entries
    return jnp.clip(entries, min=-bound, max=bound).astype(kind)


def setup_inputs(seed: int = 0) -> dict:
    seeds = jax.random.split(jax.random.key(seed), 7)
    return {
        "integrals": scatter_about(seeds[0], (NAUX, OCC * NVIRT), 0.1, 0.796875, ((0, 128),)),
        "metric": scatter_about(seeds[1], (NAUX, NAUX), NAUX ** -0.5, 0.109375, ((0, 8),)),
        "occ_energy": jnp.clip(jax.random.uniform(seeds[2], (OCC,), jnp.float32, -1.5, -0.3), -1.5, -0.3),
        "virt_energy": jnp.clip(jax.random.uniform(seeds[3], (NVIRT,), jnp.float32, 0.3, 3.0), 0.3, 3.0),
        "pair_table": draw_pair_table(jax.random.fold_in(seeds[6], 71), 0),
        "pair_count": draw_pair_count(jax.random.fold_in(seeds[6], 71), 0),
    }


def add_row(gradient, row_values, index):
    current = lax.dynamic_index_in_dim(gradient, index, 1, keepdims=False)
    return lax.dynamic_update_index_in_dim(gradient, current + row_values, index, 1)


def reference(integrals, metric, occ_energy, virt_energy, pair_table, pair_count):
    slab = NAUX // N_AUX
    fitted = jnp.zeros((NAUX, OCC * NVIRT), jnp.float32)
    for piece in range(N_AUX):
        term = lax.dot_general(metric[piece * slab:(piece + 1) * slab], integrals[piece * slab:(piece + 1) * slab], (((0,), (0,)), ((), ())), preferred_element_type=jnp.float32)
        fitted = fitted + term
    fitted_b = fitted.astype(jnp.bfloat16).reshape(NAUX, OCC, NVIRT)
    living = (jnp.arange(CAP, dtype=jnp.int32)[None, :] < pair_count[:, None]).reshape(-1)

    def visit(slot, gradient):
        occ_left = pair_table[slot, 0].astype(jnp.int32)
        occ_right = pair_table[slot, 1].astype(jnp.int32)
        left = lax.dynamic_index_in_dim(fitted_b, occ_left, 1, keepdims=False)
        right = lax.dynamic_index_in_dim(fitted_b, occ_right, 1, keepdims=False)
        pair_ints = lax.dot_general(left, right, (((0,), (0,)), ((), ())), preferred_element_type=jnp.float32)
        denominator = virt_energy[:, None] + virt_energy[None, :] - occ_energy[occ_left] - occ_energy[occ_right]
        amplitude = (pair_ints / denominator).astype(jnp.bfloat16)
        to_left = lax.dot_general(right, amplitude, (((1,), (1,)), ((), ())), preferred_element_type=jnp.float32)
        to_right = jnp.dot(left, amplitude, preferred_element_type=jnp.float32)
        gradient = add_row(gradient, to_left, occ_left)
        return add_row(gradient, to_right, occ_right)

    def skip(slot, gradient):
        return gradient

    def step(slot, gradient):
        return lax.cond(living[slot], visit, skip, slot, gradient)

    gradient = lax.fori_loop(0, SLOTS, step, jnp.zeros((NAUX, OCC, NVIRT), jnp.float32))
    return gradient.reshape(NAUX, OCC * NVIRT)
```

```python
import jax
import jax.numpy as jnp
from jax import lax
from jax.sharding import PartitionSpec as P


def on_device(integrals, metric, occ_energy, virt_energy, pair_table, pair_count):
    occ = occ_energy.shape[0]
    virt = virt_energy.shape[0]
    me = lax.axis_index("pair")
    alpha = lax.axis_index("aux")
    n_pair = lax.axis_size("pair")
    live = (jnp.arange(pair_table.shape[0]) < pair_count[0]).astype(jnp.float32)
    left = jax.nn.one_hot(pair_table[:, 0], occ, dtype=jnp.float32)
    right = jax.nn.one_hot(pair_table[:, 1], occ, dtype=jnp.float32)
    mine = jnp.einsum("s,si,sj->ij", live, left, right)
    weight = lax.psum(mine + mine.T, "pair")

    regrouped = lax.all_to_all(integrals, "pair", split_axis=1, concat_axis=0, tiled=True)
    cols = regrouped.shape[1]
    partial = lax.dot_general(regrouped, metric, (((0,), (0,)), ((), ())), preferred_element_type=jnp.float32)
    shard = lax.psum_scatter(partial, "aux", scatter_dimension=0, tiled=True).astype(jnp.bfloat16)
    width = shard.shape[0]
    keys = lax.all_gather(shard, "pair", axis=0, tiled=True)
    queries = lax.all_gather(shard, "aux", axis=0, tiled=True)
    scores = lax.dot_general(queries, keys, (((1,), (1,)), ((), ())), preferred_element_type=jnp.float32)
    query_col = me * cols + jnp.arange(cols)
    key_col = ((jnp.arange(n_pair) * cols + alpha * width)[:, None] + jnp.arange(width)[None, :]).reshape(-1)
    e_query = virt_energy[query_col % virt]
    e_key = virt_energy[key_col % virt]
    o_query = occ_energy[query_col // virt]
    o_key = occ_energy[key_col // virt]
    denominator = e_query[:, None] + e_key[None, :] - o_query[:, None] - o_key[None, :]
    amplitude = (scores / denominator).astype(jnp.bfloat16)
    row = lax.dynamic_index_in_dim(weight, me * cols // virt, 0, keepdims=False)
    per = keys.shape[0] // occ
    grad = 0.0
    for j in range(occ):
        grad = grad + row[j] * jnp.dot(
            amplitude[:, j * per:(j + 1) * per], keys[j * per:(j + 1) * per], preferred_element_type=jnp.float32
        )
    out = lax.psum_scatter(grad, "aux", scatter_dimension=1, tiled=True)
    return out.T


def solution(mesh):
    placed = (P(("aux", "pair"), None), P("aux", None), P(), P(), P("pair", None), P("pair"))
    return jax.shard_map(
        on_device, mesh=mesh, in_specs=placed, out_specs=P("aux", "pair"), check_vma=False
    )
```

```python
import functools

import jax
import jax.numpy as jnp
from jax import lax
from jax.experimental import pallas as pl
from jax.experimental.pallas import tpu as pltpu
from jax.sharding import PartitionSpec as P

MESH = pl.DeviceIdType.MESH
F32, BF16, I16 = jnp.float32, jnp.bfloat16, jnp.int16
CHUNKS = 4
LEVELS = 32000.0


def flipped_dot(a, b):
    return lax.dot_general(a, b, (((1,), (1,)), ((), ())), preferred_element_type=F32)


def encode(x):
    top = jnp.maximum(jnp.max(jnp.abs(x), axis=(0, 1), keepdims=True), 1e-30)
    return jnp.round(x * (LEVELS / top)).astype(jnp.int32).astype(I16), jnp.broadcast_to(top / LEVELS, (8, 128))


def decode(code, scale):
    return code.astype(F32) * scale[0:1, 0:1]


def kernel(ints, metric, virt, near, occ, tab, cnt, out,
           kv, qb, abuf, pbuf, mpart, flip, wbuf, wsum, pf,
           e2, s2, r2, t2, e1, s1, r1, t1,
           scores, amp, gt, gs2, gr2, gs1, gr1, gp, gpr,
           send, recv):
    p = lax.axis_index("pair")
    alpha = lax.axis_index("aux")
    z, x = p // 4, p % 4
    y, c = alpha // 2, alpha % 2
    other = 1 - c
    xl, xr = (x + 3) % 4, (x + 1) % 4
    zl, zr = (z + 3) % 4, (z + 1) % 4
    yl, yr = (y + 3) % 4, (y + 1) % 4
    naux = metric.shape[1]
    step = naux // CHUNKS
    n_pair = 16
    half = 256

    def dev(zz=z, xx=x, yy=y, cc=c):
        return {"pair": zz * 4 + xx, "aux": yy * 2 + cc}

    counter = [0]
    started = []

    def copy(src, dst, where, recv_at=None):
        at = counter[0]
        counter[0] += 1
        made = pltpu.make_async_remote_copy(
            src_ref=src, dst_ref=dst, send_sem=send.at[at],
            recv_sem=recv.at[at if recv_at is None else recv_at],
            device_id=where, device_id_type=MESH)
        made.start()
        started.append(made)
        return made

    barrier = pltpu.get_barrier_semaphore()
    peers = [{"pair": (p + d) % n_pair, "aux": alpha} for d in range(1, n_pair)]
    peers += [dev(yy=yl), dev(yy=yr), dev(yy=yl, cc=other), dev(yy=yr, cc=other), dev(cc=other)]
    for peer in peers:
        pl.semaphore_signal(barrier, inc=1, device_id=peer, device_id_type=MESH)

    row = lax.broadcasted_iota(jnp.int32, (8, 128), 0)
    lane = lax.broadcasted_iota(jnp.int32, (8, 128), 1)
    counts = jnp.zeros((8, 128), F32)
    for slot in range(2):
        i, j = tab[slot, 0], tab[slot, 1]
        live = jnp.where(cnt[0] > slot, 1.0, 0.0)
        hits = jnp.where((row == i) & (lane == j), 1.0, 0.0) + jnp.where((row == j) & (lane == i), 1.0, 0.0)
        counts = counts + live * hits
    wbuf[p] = counts
    pl.semaphore_wait(barrier, len(peers))

    gathers = []
    for d in range(1, n_pair):
        to = (p + d) % n_pair
        where = {"pair": to, "aux": alpha}
        gathers.append(copy(ints.at[:, pl.ds(pl.multiple_of(to * 512, 512), 512)], abuf.at[p], where))
    metric_copy = copy(metric, mpart, dev(cc=other))
    weights = []
    for d in range(1, n_pair):
        where = {"pair": (p + d) % n_pair, "aux": alpha}
        weights.append(copy(wbuf.at[p], wbuf.at[p], where))
    abuf[p] = ints[:, pl.ds(pl.multiple_of(p * 512, 512), 512)]
    for made in gathers:
        made.wait_recv()
    mine_cols = pl.ds(pl.multiple_of(c * half, half), half)
    other_cols = pl.ds(pl.multiple_of(other * half, half), half)
    half_copy = copy(abuf.at[:, :, other_cols], pbuf, dev(cc=other))
    rows = metric.shape[0]
    flip[0] = abuf[:, :, mine_cols].reshape(rows, half).T
    half_copy.wait_recv()
    flip[1] = pbuf[...].reshape(rows, half).T
    metric_copy.wait_recv()

    def lanes(q):
        return pl.ds(q * step, step)

    second, first = [], []
    for q in range(CHUNKS):
        pf[:, lanes(q)] = (jnp.dot(flip[0], metric[:, lanes(q)], preferred_element_type=F32)
                           + jnp.dot(flip[1], mpart[:, lanes(q)], preferred_element_type=F32))
        far = (y + 2) % 4 * 64
        made = []
        for side, to in ((0, yl), (1, yr)):
            code, scale = encode(pf[pl.ds(pl.multiple_of(far + side * 32, 32), 32), lanes(q)])
            e2[side, :, lanes(q)] = code
            s2[q, side] = scale
            made.append((copy(e2.at[side, :, lanes(q)], r2.at[side, :, lanes(q)], dev(yy=to)),
                         copy(s2.at[q, side], t2.at[q, side], dev(yy=to))))
        second.append(made)

    def pass_on(q):
        made = []
        for side, to in ((0, yl), (1, yr)):
            for item in second[q][side]:
                item.wait_recv()
            block = pf[pl.ds(pl.multiple_of(to * 64, 64), 64), lanes(q)]
            got = decode(r2[side, :, lanes(q)], t2[q, side])
            zero = jnp.zeros_like(got)
            block = block + jnp.concatenate([got, zero] if side == 0 else [zero, got], axis=0)
            code, scale = encode(block)
            e1[side, :, lanes(q)] = code
            s1[q, side] = scale
            made.append((copy(e1.at[side, :, lanes(q)], r1.at[side, :, lanes(q)], dev(yy=to)),
                         copy(s1.at[q, side], t1.at[q, side], dev(yy=to))))
        first.append(made)

    flight = {}

    def begin(q):
        for side in range(2):
            for item in first[q][side]:
                item.wait_recv()
        total = pf[pl.ds(pl.multiple_of(y * 64, 64), 64), lanes(q)]
        for side in range(2):
            total = total + decode(r1[side, :, lanes(q)], t1[q, side])
        fitted = total.astype(BF16)
        kv[z, x, c, :, lanes(q)] = fitted
        qb[y, :, lanes(q)] = fitted
        top, low = pl.ds(0, 32), pl.ds(32, 32)
        mine_top = kv.at[z, x, c, top, lanes(q)]
        mine_low = kv.at[z, x, c, low, lanes(q)]
        mine_q = qb.at[y, :, lanes(q)]
        flight["x1", q] = (copy(mine_top, mine_top, dev(xx=xl)), copy(mine_top, mine_top, dev(xx=xr)))
        flight["z1", q] = (copy(mine_low, mine_low, dev(zz=zl)), copy(mine_low, mine_low, dev(zz=zr)))
        flight["q1", q] = (copy(mine_q, mine_q, dev(yy=yl)), copy(mine_q, mine_q, dev(yy=yr)))

    def relay(q):
        toward_left, toward_right = flight["x1", q]
        toward_right.wait_recv()
        piece = kv.at[z, xl, c, pl.ds(0, 16), lanes(q)]
        right = copy(piece, piece, dev(xx=xr))
        toward_left.wait_recv()
        piece = kv.at[z, xr, c, pl.ds(16, 16), lanes(q)]
        flight["x2", q] = (copy(piece, piece, dev(xx=xl)), right)
        toward_left, toward_right = flight["z1", q]
        toward_right.wait_recv()
        piece = kv.at[zl, x, c, pl.ds(32, 16), lanes(q)]
        right = copy(piece, piece, dev(zz=zr))
        toward_left.wait_recv()
        piece = kv.at[zr, x, c, pl.ds(48, 16), lanes(q)]
        flight["z2", q] = (copy(piece, piece, dev(zz=zl)), right)
        toward_left, toward_right = flight["q1", q]
        toward_right.wait_recv()
        piece = qb.at[yl, pl.ds(0, 32), lanes(q)]
        right = copy(piece, piece, dev(yy=yr))
        toward_left.wait_recv()
        piece = qb.at[yr, pl.ds(32, 32), lanes(q)]
        flight["q2", q] = (copy(piece, piece, dev(yy=yl)), right)

    def widen(q):
        for made in flight["x2", q]:
            made.wait_recv()
        line = kv.at[z, :, c, pl.ds(0, 32), lanes(q)]
        flight["z3", q] = (copy(line, line, dev(zz=zl)), copy(line, line, dev(zz=zr)))
        for made in flight["z2", q]:
            made.wait_recv()
        line = kv.at[:, x, c, pl.ds(32, 32), lanes(q)]
        flight["x3", q] = (copy(line, line, dev(xx=xl)), copy(line, line, dev(xx=xr)))

    def relay_lines(q):
        toward_left, toward_right = flight["z3", q]
        toward_right.wait_recv()
        line = kv.at[zl, pl.ds(0, 2), c, pl.ds(0, 32), lanes(q)]
        right = copy(line, line, dev(zz=zr))
        toward_left.wait_recv()
        line = kv.at[zr, pl.ds(2, 2), c, pl.ds(0, 32), lanes(q)]
        flight["z4", q] = (copy(line, line, dev(zz=zl)), right)
        toward_left, toward_right = flight["x3", q]
        toward_right.wait_recv()
        line = kv.at[pl.ds(0, 2), xl, c, pl.ds(32, 32), lanes(q)]
        right = copy(line, line, dev(xx=xr))
        toward_left.wait_recv()
        line = kv.at[pl.ds(2, 2), xr, c, pl.ds(32, 32), lanes(q)]
        flight["x4", q] = (copy(line, line, dev(xx=xl)), right)

    def share(q):
        for made in flight["z4", q] + flight["x4", q]:
            made.wait_recv()
        plane = kv.at[:, :, c, :, lanes(q)]
        flight["core", q] = copy(plane, plane, dev(cc=other))

    def score(q):
        for made in flight["q2", q]:
            made.wait_recv()
        flight["core", q].wait_recv()
        queries = qb[:, :, lanes(q)].reshape(half, step)

        @pl.loop(0, 8)
        def _(j):
            keys = kv[j // 2, pl.ds(j % 2 * 2, 2), :, :, lanes(q)].reshape(half, step)
            part = flipped_dot(queries, keys)
            if q == 0:
                scores[j] = part
            else:
                scores[j] = scores[j] + part

    pass_on(0)
    begin(0)
    relay(0)
    widen(0)
    for q in range(CHUNKS):
        more = q + 1 < CHUNKS
        if more:
            pass_on(q + 1)
            begin(q + 1)
        relay_lines(q)
        if more:
            relay(q + 1)
            widen(q + 1)
        share(q)
        if q > 0:
            score(q - 1)
    score(CHUNKS - 1)

    for made in weights:
        made.wait_recv()
    wsum[...] = jnp.sum(wbuf[...], axis=0)
    mine_occ = p // 2
    wrow = wsum[pl.ds(mine_occ, 1), :]

    from_virt = virt[:, pl.ds(pl.multiple_of(x % 2 * 512 + c * half, half), half)] - occ[mine_occ]
    query_e = jnp.broadcast_to(from_virt, (8, half)).T[:, 0:1]
    for j in range(8):
        key_e = near[...] - occ[j]
        amp[j] = (scores[j] / (query_e + key_e)).astype(BF16)

    piece = naux // 8

    def gradient(at, slot):
        where = pl.ds(pl.multiple_of(at * piece, 128), piece)
        total = None
        for j in range(8):
            keys = kv[j // 2, pl.ds(j % 2 * 2, 2), :, :, where].reshape(half, piece)
            part = wrow[:, j:j + 1] * jnp.dot(amp[j], keys, preferred_element_type=F32)
            total = part if total is None else total + part
        gt[slot] = total

    far_made = []
    for cc in range(2):
        gradient((y + 2) % 4 * 2 + cc, cc)
        made = []
        for side, to in ((0, yl), (1, yr)):
            gs2[side, cc] = gt[cc, pl.ds(side * 128, 128), :].astype(BF16)
            made.append(copy(gs2.at[side, cc], gr2.at[side, cc], dev(yy=to)))
        far_made.append(made)
    base = counter[0]
    near_made = []
    for cc in range(2):
        for side, to in ((0, yl), (1, yr)):
            gradient(to * 2 + cc, side)
        for side, to in ((0, yl), (1, yr)):
            far_made[cc][side].wait_recv()
            add = pl.ds(side * 128, 128)
            gt[side, add, :] = gt[side, add, :] + gr2[side, cc].astype(F32)
            gs1[side, cc] = gt[side].astype(BF16)
            near_made.append(copy(gs1.at[side, cc], gr1.at[side, c], dev(yy=to, cc=cc), recv_at=base + side * 2 + c))
    gradient(y * 2 + other, 0)
    gp[...] = gt[0].astype(BF16)
    core_made = copy(gp, gpr, dev(cc=other))
    gradient(y * 2 + c, 1)

    for side in range(2):
        for core in range(2):
            pltpu.make_async_remote_copy(
                src_ref=gs1.at[side, core], dst_ref=gr1.at[side, core], send_sem=send.at[base],
                recv_sem=recv.at[base + side * 2 + core], device_id=dev(cc=other), device_id_type=MESH).wait_recv()
    core_made.wait_recv()
    mine = gt[1] + gr1[0, c].astype(F32) + gr1[1, c].astype(F32)
    out[:, mine_cols] = mine.T
    theirs = gpr[...].astype(F32) + gr1[0, other].astype(F32) + gr1[1, other].astype(F32)
    out[:, other_cols] = theirs.T
    for made in started:
        made.wait_send()
    assert counter[0] <= send.shape[0]


COPIES = 192


def on_device(integrals, metric, occ_energy, virt_energy, pair_table, pair_count):
    naux = metric.shape[1]
    y = lax.axis_index("aux") // 2
    near = lax.dynamic_index_in_dim(virt_energy.reshape(4, 4, 64), y, 1, keepdims=False).reshape(1, 256)
    vm = pl.BlockSpec(memory_space=pltpu.VMEM)
    sm = pl.BlockSpec(memory_space=pltpu.SMEM)
    V = pltpu.VMEM
    return pl.pallas_call(
        kernel,
        out_shape=jax.ShapeDtypeStruct((384, 512), F32),
        in_specs=[vm, vm, vm, vm, sm, sm, sm],
        out_specs=vm,
        scratch_shapes=[
            V((4, 4, 2, 64, naux), BF16),
            V((4, 64, naux), BF16),
            V((16, 24, 512), BF16),
            V((16, 24, 256), BF16),
            V((384, naux), BF16),
            V((2, 256, 384), BF16),
            V((16, 8, 128), F32),
            V((8, 128), F32),
            V((256, naux), F32),
            V((2, 32, naux), I16), V((CHUNKS, 2, 8, 128), F32), V((2, 32, naux), I16), V((CHUNKS, 2, 8, 128), F32),
            V((2, 64, naux), I16), V((CHUNKS, 2, 8, 128), F32), V((2, 64, naux), I16), V((CHUNKS, 2, 8, 128), F32),
            V((8, 256, 256), F32),
            V((8, 256, 256), BF16),
            V((2, 256, 384), F32),
            V((2, 2, 128, 384), BF16), V((2, 2, 128, 384), BF16),
            V((2, 2, 256, 384), BF16), V((2, 2, 256, 384), BF16),
            V((256, 384), BF16), V((256, 384), BF16),
            pltpu.SemaphoreType.DMA((COPIES,)),
            pltpu.SemaphoreType.DMA((COPIES,)),
        ],
        compiler_params=pltpu.CompilerParams(
            collective_id=0, has_side_effects=True, vmem_limit_bytes=60 * 1024 * 1024),
    )(integrals, metric, virt_energy.reshape(1, -1), near, occ_energy, pair_table, pair_count)


def solution(mesh):
    placed = (P(("aux", "pair"), None), P("aux", None), P(), P(), P("pair", None), P("pair"))
    return jax.shard_map(
        on_device, mesh=mesh, in_specs=placed, out_specs=P("aux", "pair"), check_vma=False
    )
```

```python
import functools

import jax
import jax.numpy as jnp
from jax import lax
from jax.experimental import pallas as pl
from jax.experimental.pallas import tpu as pltpu
from jax.sharding import PartitionSpec as P

MESH = pl.DeviceIdType.MESH
F32, BF16, I16 = jnp.float32, jnp.bfloat16, jnp.int16
CHUNKS = 4
LEVELS = 32000.0


def flipped_dot(a, b):
    return lax.dot_general(a, b, (((1,), (1,)), ((), ())), preferred_element_type=F32)


def encode(x):
    top = jnp.maximum(jnp.max(jnp.abs(x), axis=(0, 1), keepdims=True), 1e-30)
    return jnp.round(x * (LEVELS / top)).astype(jnp.int32).astype(I16), jnp.broadcast_to(top / LEVELS, (8, 128))


def decode(code, scale):
    return code.astype(F32) * scale[0:1, 0:1]


def kernel(ints, metric, virt, near, occ, tab, cnt, out,
           kv, qb, abuf, pbuf, mpart, flip, wbuf, wsum, pf,
           e2, s2, r2, t2, e1, s1, r1, t1,
           scores, amp, gt, gs2, gr2, gs1, gr1, gp, gpr,
           send, recv):
    p = lax.axis_index("pair")
    alpha = lax.axis_index("aux")
    z, x = p // 4, p % 4
    y, c = alpha // 2, alpha % 2
    other = 1 - c
    xl, xr = (x + 3) % 4, (x + 1) % 4
    zl, zr = (z + 3) % 4, (z + 1) % 4
    yl, yr = (y + 3) % 4, (y + 1) % 4
    naux = metric.shape[1]
    step = naux // CHUNKS
    n_pair = 16
    half = 256

    def dev(zz=z, xx=x, yy=y, cc=c):
        return {"pair": zz * 4 + xx, "aux": yy * 2 + cc}

    counter = [0]
    started = []

    def copy(src, dst, where, recv_at=None):
        at = counter[0]
        counter[0] += 1
        made = pltpu.make_async_remote_copy(
            src_ref=src, dst_ref=dst, send_sem=send.at[at],
            recv_sem=recv.at[at if recv_at is None else recv_at],
            device_id=where, device_id_type=MESH)
        made.start()
        started.append(made)
        return made

    barrier = pltpu.get_barrier_semaphore()
    peers = [{"pair": (p + d) % n_pair, "aux": alpha} for d in range(1, n_pair)]
    peers += [dev(yy=yl), dev(yy=yr), dev(yy=yl, cc=other), dev(yy=yr, cc=other), dev(cc=other)]
    for peer in peers:
        pl.semaphore_signal(barrier, inc=1, device_id=peer, device_id_type=MESH)

    row = lax.broadcasted_iota(jnp.int32, (8, 128), 0)
    lane = lax.broadcasted_iota(jnp.int32, (8, 128), 1)
    counts = jnp.zeros((8, 128), F32)
    for slot in range(2):
        i, j = tab[slot, 0], tab[slot, 1]
        live = jnp.where(cnt[0] > slot, 1.0, 0.0)
        hits = jnp.where((row == i) & (lane == j), 1.0, 0.0) + jnp.where((row == j) & (lane == i), 1.0, 0.0)
        counts = counts + live * hits
    wbuf[p] = counts
    pl.semaphore_wait(barrier, len(peers))

    gathers = []
    for d in range(1, n_pair):
        to = (p + d) % n_pair
        where = {"pair": to, "aux": alpha}
        gathers.append(copy(ints.at[:, pl.ds(pl.multiple_of(to * 512, 512), 512)], abuf.at[p], where))
    metric_copy = copy(metric, mpart, dev(cc=other))
    weights = []
    for d in range(1, n_pair):
        where = {"pair": (p + d) % n_pair, "aux": alpha}
        weights.append(copy(wbuf.at[p], wbuf.at[p], where))
    abuf[p] = ints[:, pl.ds(pl.multiple_of(p * 512, 512), 512)]
    for made in gathers:
        made.wait_recv()
    mine_cols = pl.ds(pl.multiple_of(c * half, half), half)
    other_cols = pl.ds(pl.multiple_of(other * half, half), half)
    half_copy = copy(abuf.at[:, :, other_cols], pbuf, dev(cc=other))
    rows = metric.shape[0]
    flip[0] = abuf[:, :, mine_cols].reshape(rows, half).T
    half_copy.wait_recv()
    flip[1] = pbuf[...].reshape(rows, half).T
    metric_copy.wait_recv()

    def lanes(q):
        return pl.ds(q * step, step)

    second, first = [], []
    for q in range(CHUNKS):
        pf[:, lanes(q)] = (jnp.dot(flip[0], metric[:, lanes(q)], preferred_element_type=F32)
                           + jnp.dot(flip[1], mpart[:, lanes(q)], preferred_element_type=F32))
        far = (y + 2) % 4 * 64
        made = []
        for side, to in ((0, yl), (1, yr)):
            code, scale = encode(pf[pl.ds(pl.multiple_of(far + side * 32, 32), 32), lanes(q)])
            e2[side, :, lanes(q)] = code
            s2[q, side] = scale
            made.append((copy(e2.at[side, :, lanes(q)], r2.at[side, :, lanes(q)], dev(yy=to)),
                         copy(s2.at[q, side], t2.at[q, side], dev(yy=to))))
        second.append(made)

    def pass_on(q):
        made = []
        for side, to in ((0, yl), (1, yr)):
            for item in second[q][side]:
                item.wait_recv()
            block = pf[pl.ds(pl.multiple_of(to * 64, 64), 64), lanes(q)]
            got = decode(r2[side, :, lanes(q)], t2[q, side])
            zero = jnp.zeros_like(got)
            block = block + jnp.concatenate([got, zero] if side == 0 else [zero, got], axis=0)
            code, scale = encode(block)
            e1[side, :, lanes(q)] = code
            s1[q, side] = scale
            made.append((copy(e1.at[side, :, lanes(q)], r1.at[side, :, lanes(q)], dev(yy=to)),
                         copy(s1.at[q, side], t1.at[q, side], dev(yy=to))))
        first.append(made)

    flight = {}

    def begin(q):
        for side in range(2):
            for item in first[q][side]:
                item.wait_recv()
        total = pf[pl.ds(pl.multiple_of(y * 64, 64), 64), lanes(q)]
        for side in range(2):
            total = total + decode(r1[side, :, lanes(q)], t1[q, side])
        fitted = total.astype(BF16)
        kv[z, x, c, :, lanes(q)] = fitted
        qb[y, :, lanes(q)] = fitted
        top, low = pl.ds(0, 32), pl.ds(32, 32)
        mine_top = kv.at[z, x, c, top, lanes(q)]
        mine_low = kv.at[z, x, c, low, lanes(q)]
        mine_q = qb.at[y, :, lanes(q)]
        flight["x1", q] = (copy(mine_top, mine_top, dev(xx=xl)), copy(mine_top, mine_top, dev(xx=xr)))
        flight["z1", q] = (copy(mine_low, mine_low, dev(zz=zl)), copy(mine_low, mine_low, dev(zz=zr)))
        flight["q1", q] = (copy(mine_q, mine_q, dev(yy=yl)), copy(mine_q, mine_q, dev(yy=yr)))

    def relay(q):
        toward_left, toward_right = flight["x1", q]
        toward_right.wait_recv()
        piece = kv.at[z, xl, c, pl.ds(0, 16), lanes(q)]
        right = copy(piece, piece, dev(xx=xr))
        toward_left.wait_recv()
        piece = kv.at[z, xr, c, pl.ds(16, 16), lanes(q)]
        flight["x2", q] = (copy(piece, piece, dev(xx=xl)), right)
        toward_left, toward_right = flight["z1", q]
        toward_right.wait_recv()
        piece = kv.at[zl, x, c, pl.ds(32, 16), lanes(q)]
        right = copy(piece, piece, dev(zz=zr))
        toward_left.wait_recv()
        piece = kv.at[zr, x, c, pl.ds(48, 16), lanes(q)]
        flight["z2", q] = (copy(piece, piece, dev(zz=zl)), right)
        toward_left, toward_right = flight["q1", q]
        toward_right.wait_recv()
        piece = qb.at[yl, pl.ds(0, 32), lanes(q)]
        right = copy(piece, piece, dev(yy=yr))
        toward_left.wait_recv()
        piece = qb.at[yr, pl.ds(32, 32), lanes(q)]
        flight["q2", q] = (copy(piece, piece, dev(yy=yl)), right)

    def widen(q):
        for made in flight["x2", q]:
            made.wait_recv()
        line = kv.at[z, :, c, pl.ds(0, 32), lanes(q)]
        flight["z3", q] = (copy(line, line, dev(zz=zl)), copy(line, line, dev(zz=zr)))
        for made in flight["z2", q]:
            made.wait_recv()
        line = kv.at[:, x, c, pl.ds(32, 32), lanes(q)]
        flight["x3", q] = (copy(line, line, dev(xx=xl)), copy(line, line, dev(xx=xr)))

    def relay_lines(q):
        toward_left, toward_right = flight["z3", q]
        toward_right.wait_recv()
        line = kv.at[zl, pl.ds(0, 2), c, pl.ds(0, 32), lanes(q)]
        right = copy(line, line, dev(zz=zr))
        toward_left.wait_recv()
        line = kv.at[zr, pl.ds(2, 2), c, pl.ds(0, 32), lanes(q)]
        flight["z4", q] = (copy(line, line, dev(zz=zl)), right)
        toward_left, toward_right = flight["x3", q]
        toward_right.wait_recv()
        line = kv.at[pl.ds(0, 2), xl, c, pl.ds(32, 32), lanes(q)]
        right = copy(line, line, dev(xx=xr))
        toward_left.wait_recv()
        line = kv.at[pl.ds(2, 2), xr, c, pl.ds(32, 32), lanes(q)]
        flight["x4", q] = (copy(line, line, dev(xx=xl)), right)

    def share(q):
        made = []
        for zz in (z, zl, zr):
            line = kv.at[zz, :, c, pl.ds(0, 32), lanes(q)]
            made.append(copy(line, line, dev(cc=other)))
        for xx in (x, xl, xr):
            line = kv.at[:, xx, c, pl.ds(32, 32), lanes(q)]
            made.append(copy(line, line, dev(cc=other)))
        flight["core", q] = made

    def share_far(q):
        for made in flight["z4", q] + flight["x4", q]:
            made.wait_recv()
        line = kv.at[(z + 2) % 4, :, c, pl.ds(0, 32), lanes(q)]
        flight["core", q].append(copy(line, line, dev(cc=other)))
        line = kv.at[:, (x + 2) % 4, c, pl.ds(32, 32), lanes(q)]
        flight["core", q].append(copy(line, line, dev(cc=other)))

    def score(q):
        for made in flight["q2", q]:
            made.wait_recv()
        for made in flight["core", q]:
            made.wait_recv()
        queries = qb[:, :, lanes(q)].reshape(half, step)

        @pl.loop(0, 8)
        def _(j):
            keys = kv[j // 2, pl.ds(j % 2 * 2, 2), :, :, lanes(q)].reshape(half, step)
            part = flipped_dot(queries, keys)
            if q == 0:
                scores[j] = part
            else:
                scores[j] = scores[j] + part

    stages = ((pass_on, -1.5), (begin, 1.2), (relay, 2.3), (widen, 3.4), (relay_lines, 5.5), (share, 5.55), (share_far, 7.6), (score, 9.7))
    order = [(at + 2 * q, q, run) for run, at in stages for q in range(CHUNKS)]
    for _, q, run in sorted(order, key=lambda item: item[:2]):
        run(q)

    for made in weights:
        made.wait_recv()
    wsum[...] = jnp.sum(wbuf[...], axis=0)
    mine_occ = p // 2
    wrow = wsum[pl.ds(mine_occ, 1), :]

    from_virt = virt[:, pl.ds(pl.multiple_of(x % 2 * 512 + c * half, half), half)] - occ[mine_occ]
    query_e = jnp.broadcast_to(from_virt, (8, half)).T[:, 0:1]
    for j in range(8):
        key_e = near[...] - occ[j]
        amp[j] = (scores[j] / (query_e + key_e)).astype(BF16)

    piece = naux // 8

    def gradient(at, slot):
        where = pl.ds(pl.multiple_of(at * piece, 128), piece)
        total = None
        for j in range(8):
            keys = kv[j // 2, pl.ds(j % 2 * 2, 2), :, :, where].reshape(half, piece)
            part = wrow[:, j:j + 1] * jnp.dot(amp[j], keys, preferred_element_type=F32)
            total = part if total is None else total + part
        gt[slot] = total

    far_made = []
    for cc in range(2):
        gradient((y + 2) % 4 * 2 + cc, cc)
        made = []
        for side, to in ((0, yl), (1, yr)):
            gs2[side, cc] = gt[cc, pl.ds(side * 128, 128), :].astype(BF16)
            made.append(copy(gs2.at[side, cc], gr2.at[side, cc], dev(yy=to)))
        far_made.append(made)
    base = counter[0]
    near_made = []
    for cc in range(2):
        for side, to in ((0, yl), (1, yr)):
            gradient(to * 2 + cc, side)
        for side, to in ((0, yl), (1, yr)):
            far_made[cc][side].wait_recv()
            add = pl.ds(side * 128, 128)
            gt[side, add, :] = gt[side, add, :] + gr2[side, cc].astype(F32)
            gs1[side, cc] = gt[side].astype(BF16)
            near_made.append(copy(gs1.at[side, cc], gr1.at[side, c], dev(yy=to, cc=cc), recv_at=base + side * 2 + c))
    gradient(y * 2 + other, 0)
    gp[...] = gt[0].astype(BF16)
    core_made = copy(gp, gpr, dev(cc=other))
    gradient(y * 2 + c, 1)

    for side in range(2):
        for core in range(2):
            pltpu.make_async_remote_copy(
                src_ref=gs1.at[side, core], dst_ref=gr1.at[side, core], send_sem=send.at[base],
                recv_sem=recv.at[base + side * 2 + core], device_id=dev(cc=other), device_id_type=MESH).wait_recv()
    core_made.wait_recv()
    mine = gt[1] + gr1[0, c].astype(F32) + gr1[1, c].astype(F32)
    out[:, mine_cols] = mine.T
    theirs = gpr[...].astype(F32) + gr1[0, other].astype(F32) + gr1[1, other].astype(F32)
    out[:, other_cols] = theirs.T
    for made in started:
        made.wait_send()
    assert counter[0] <= send.shape[0]


COPIES = 256


def on_device(integrals, metric, occ_energy, virt_energy, pair_table, pair_count):
    naux = metric.shape[1]
    y = lax.axis_index("aux") // 2
    near = lax.dynamic_index_in_dim(virt_energy.reshape(4, 4, 64), y, 1, keepdims=False).reshape(1, 256)
    vm = pl.BlockSpec(memory_space=pltpu.VMEM)
    sm = pl.BlockSpec(memory_space=pltpu.SMEM)
    V = pltpu.VMEM
    return pl.pallas_call(
        kernel,
        out_shape=jax.ShapeDtypeStruct((384, 512), F32),
        in_specs=[vm, vm, vm, vm, sm, sm, sm],
        out_specs=vm,
        scratch_shapes=[
            V((4, 4, 2, 64, naux), BF16),
            V((4, 64, naux), BF16),
            V((16, 24, 512), BF16),
            V((16, 24, 256), BF16),
            V((384, naux), BF16),
            V((2, 256, 384), BF16),
            V((16, 8, 128), F32),
            V((8, 128), F32),
            V((256, naux), F32),
            V((2, 32, naux), I16), V((CHUNKS, 2, 8, 128), F32), V((2, 32, naux), I16), V((CHUNKS, 2, 8, 128), F32),
            V((2, 64, naux), I16), V((CHUNKS, 2, 8, 128), F32), V((2, 64, naux), I16), V((CHUNKS, 2, 8, 128), F32),
            V((8, 256, 256), F32),
            V((8, 256, 256), BF16),
            V((2, 256, 384), F32),
            V((2, 2, 128, 384), BF16), V((2, 2, 128, 384), BF16),
            V((2, 2, 256, 384), BF16), V((2, 2, 256, 384), BF16),
            V((256, 384), BF16), V((256, 384), BF16),
            pltpu.SemaphoreType.DMA((COPIES,)),
            pltpu.SemaphoreType.DMA((COPIES,)),
        ],
        compiler_params=pltpu.CompilerParams(
            collective_id=0, has_side_effects=True, vmem_limit_bytes=60 * 1024 * 1024),
    )(integrals, metric, virt_energy.reshape(1, -1), near, occ_energy, pair_table, pair_count)


def solution(mesh):
    placed = (P(("aux", "pair"), None), P("aux", None), P(), P(), P("pair", None), P("pair"))
    return jax.shard_map(
        on_device, mesh=mesh, in_specs=placed, out_specs=P("aux", "pair"), check_vma=False
    )
```

```python
import functools

import jax
import jax.numpy as jnp
from jax import lax
from jax.experimental import pallas as pl
from jax.experimental.pallas import tpu as pltpu
from jax.sharding import PartitionSpec as P

MESH = pl.DeviceIdType.MESH
F32, BF16, I16 = jnp.float32, jnp.bfloat16, jnp.int16
CHUNKS = 3
FIT, PASS = (-8, 1), (-5.5, 1)
BEGIN, RELAY, WIDEN = (1.2, 0.9), (2.2, 0.9), (3.3, 2)
ASK, REASK = (1.25, 0.9), (5.2, 2)
LINES, SHARE, FAR, SCORE = (5.5, 2), (5.55, 2), (7.6, 2), (9.7, 2)
LEVELS = 32000.0


def encode(x):
    top = jnp.maximum(jnp.max(jnp.abs(x), axis=(0, 1), keepdims=True), 1e-30)
    return jnp.round(x * (LEVELS / top)).astype(jnp.int32).astype(I16), jnp.broadcast_to(top / LEVELS, (8, 128))


def decode(code, scale):
    return code.astype(F32) * scale[0:1, 0:1]


def kernel(ints, metric, virt, near, occ, tab, cnt, out,
           kv, qb, abuf, pbuf, mfull, flip, wbuf, wsum, pf,
           e2, s2, r2, t2, e1, s1, r1, t1,
           turned, scores, amp, gt, gs2, gr2, gs1, gr1, gp, gpr,
           send, recv, local):
    p = lax.axis_index("pair")
    alpha = lax.axis_index("aux")
    z, x = p // 4, p % 4
    y, c = alpha // 2, alpha % 2
    other = 1 - c
    xl, xr = (x + 3) % 4, (x + 1) % 4
    zl, zr = (z + 3) % 4, (z + 1) % 4
    yl, yr = (y + 3) % 4, (y + 1) % 4
    naux = metric.shape[1]
    step = naux // CHUNKS
    n_pair = 16
    half = 256

    def dev(zz=z, xx=x, yy=y, cc=c):
        return {"pair": zz * 4 + xx, "aux": yy * 2 + cc}

    counter = [0]
    started = []

    def copy(src, dst, where, recv_at=None):
        at = counter[0]
        counter[0] += 1
        made = pltpu.make_async_remote_copy(
            src_ref=src, dst_ref=dst, send_sem=send.at[at],
            recv_sem=recv.at[at if recv_at is None else recv_at],
            device_id=where, device_id_type=MESH)
        made.start()
        started.append(made)
        return made

    barrier = pltpu.get_barrier_semaphore()
    peers = [{"pair": (p + d) % n_pair, "aux": alpha} for d in range(1, n_pair)]
    peers += [dev(yy=yl), dev(yy=yr), dev(yy=yl, cc=other), dev(yy=yr, cc=other), dev(cc=other)]
    for peer in peers:
        pl.semaphore_signal(barrier, inc=1, device_id=peer, device_id_type=MESH)

    row = lax.broadcasted_iota(jnp.int32, (8, 128), 0)
    lane = lax.broadcasted_iota(jnp.int32, (8, 128), 1)
    counts = jnp.zeros((8, 128), F32)
    for slot in range(2):
        i, j = tab[slot, 0], tab[slot, 1]
        live = jnp.where(cnt[0] > slot, 1.0, 0.0)
        hits = jnp.where((row == i) & (lane == j), 1.0, 0.0) + jnp.where((row == j) & (lane == i), 1.0, 0.0)
        counts = counts + live * hits
    wbuf[p] = counts
    own_metric = pltpu.make_async_copy(metric, mfull.at[0], local)
    own_metric.start()
    pl.semaphore_wait(barrier, len(peers))

    gathers = []
    for d in range(1, n_pair):
        to = (p + d) % n_pair
        where = {"pair": to, "aux": alpha}
        gathers.append(copy(ints.at[:, pl.ds(pl.multiple_of(to * 512, 512), 512)], abuf.at[p], where))
    metric_copy = copy(metric, mfull.at[1], dev(cc=other))
    weights = []
    for d in range(1, n_pair):
        where = {"pair": (p + d) % n_pair, "aux": alpha}
        weights.append(copy(wbuf.at[p], wbuf.at[p], where))
    abuf[p] = ints[:, pl.ds(pl.multiple_of(p * 512, 512), 512)]
    for made in gathers:
        made.wait_recv()
    mine_cols = pl.ds(pl.multiple_of(c * half, half), half)
    other_cols = pl.ds(pl.multiple_of(other * half, half), half)
    half_copy = copy(abuf.at[:, :, other_cols], pbuf, dev(cc=other))
    rows = metric.shape[0]
    flip[:, 0:rows] = abuf[:, :, mine_cols].reshape(rows, half).T
    half_copy.wait_recv()
    flip[:, rows:2 * rows] = pbuf[...].reshape(rows, half).T
    own_metric.wait()
    metric_copy.wait_recv()

    def lanes(q):
        return pl.ds(q * step, step)

    second, first = [None] * CHUNKS, [None] * CHUNKS

    def fit(q):
        pf[:, lanes(q)] = jnp.dot(
            flip[...], mfull[:, :, lanes(q)].reshape(2 * rows, step), preferred_element_type=F32)
        far = (y + 2) % 4 * 64
        made = []
        for side, to in ((0, yl), (1, yr)):
            code, scale = encode(pf[pl.ds(pl.multiple_of(far + side * 32, 32), 32), lanes(q)])
            e2[side, :, lanes(q)] = code
            s2[q, side] = scale
            made.append((copy(e2.at[side, :, lanes(q)], r2.at[side, :, lanes(q)], dev(yy=to)),
                         copy(s2.at[q, side], t2.at[q, side], dev(yy=to))))
        second[q] = made

    def pass_on(q):
        made = []
        for side, to in ((0, yl), (1, yr)):
            for item in second[q][side]:
                item.wait_recv()
            block = pf[pl.ds(pl.multiple_of(to * 64, 64), 64), lanes(q)]
            got = decode(r2[side, :, lanes(q)], t2[q, side])
            zero = jnp.zeros_like(got)
            block = block + jnp.concatenate([got, zero] if side == 0 else [zero, got], axis=0)
            code, scale = encode(block)
            e1[side, :, lanes(q)] = code
            s1[q, side] = scale
            made.append((copy(e1.at[side, :, lanes(q)], r1.at[side, :, lanes(q)], dev(yy=to)),
                         copy(s1.at[q, side], t1.at[q, side], dev(yy=to))))
        first[q] = made

    flight = {}

    def begin(q):
        for side in range(2):
            for item in first[q][side]:
                item.wait_recv()
        total = pf[pl.ds(pl.multiple_of(y * 64, 64), 64), lanes(q)]
        for side in range(2):
            total = total + decode(r1[side, :, lanes(q)], t1[q, side])
        fitted = total.astype(BF16)
        kv[z, x, c, :, lanes(q)] = fitted
        qb[y, :, lanes(q)] = fitted
        top, low = pl.ds(0, 32), pl.ds(32, 32)
        mine_top = kv.at[z, x, c, top, lanes(q)]
        mine_low = kv.at[z, x, c, low, lanes(q)]
        flight["x1", q] = (copy(mine_top, mine_top, dev(xx=xl)), copy(mine_top, mine_top, dev(xx=xr)))
        flight["z1", q] = (copy(mine_low, mine_low, dev(zz=zl)), copy(mine_low, mine_low, dev(zz=zr)))

    def relay(q):
        toward_left, toward_right = flight["x1", q]
        toward_right.wait_recv()
        piece = kv.at[z, xl, c, pl.ds(0, 16), lanes(q)]
        right = copy(piece, piece, dev(xx=xr))
        toward_left.wait_recv()
        piece = kv.at[z, xr, c, pl.ds(16, 16), lanes(q)]
        flight["x2", q] = (copy(piece, piece, dev(xx=xl)), right)
        toward_left, toward_right = flight["z1", q]
        toward_right.wait_recv()
        piece = kv.at[zl, x, c, pl.ds(32, 16), lanes(q)]
        right = copy(piece, piece, dev(zz=zr))
        toward_left.wait_recv()
        piece = kv.at[zr, x, c, pl.ds(48, 16), lanes(q)]
        flight["z2", q] = (copy(piece, piece, dev(zz=zl)), right)

    def ask(q):
        mine_q = qb.at[y, :, lanes(q)]
        flight["q1", q] = (copy(mine_q, mine_q, dev(yy=yl)), copy(mine_q, mine_q, dev(yy=yr)))

    def relay_ask(q):
        toward_left, toward_right = flight["q1", q]
        toward_right.wait_recv()
        piece = qb.at[yl, pl.ds(0, 32), lanes(q)]
        right = copy(piece, piece, dev(yy=yr))
        toward_left.wait_recv()
        piece = qb.at[yr, pl.ds(32, 32), lanes(q)]
        flight["q2", q] = (copy(piece, piece, dev(yy=yl)), right)

    def widen(q):
        for made in flight["x2", q]:
            made.wait_recv()
        line = kv.at[z, :, c, pl.ds(0, 32), lanes(q)]
        flight["z3", q] = (copy(line, line, dev(zz=zl)), copy(line, line, dev(zz=zr)))
        for made in flight["z2", q]:
            made.wait_recv()
        line = kv.at[:, x, c, pl.ds(32, 32), lanes(q)]
        flight["x3", q] = (copy(line, line, dev(xx=xl)), copy(line, line, dev(xx=xr)))

    def relay_lines(q):
        toward_left, toward_right = flight["z3", q]
        toward_right.wait_recv()
        line = kv.at[zl, pl.ds(0, 2), c, pl.ds(0, 32), lanes(q)]
        right = copy(line, line, dev(zz=zr))
        toward_left.wait_recv()
        line = kv.at[zr, pl.ds(2, 2), c, pl.ds(0, 32), lanes(q)]
        flight["z4", q] = (copy(line, line, dev(zz=zl)), right)
        toward_left, toward_right = flight["x3", q]
        toward_right.wait_recv()
        line = kv.at[pl.ds(0, 2), xl, c, pl.ds(32, 32), lanes(q)]
        right = copy(line, line, dev(xx=xr))
        toward_left.wait_recv()
        line = kv.at[pl.ds(2, 2), xr, c, pl.ds(32, 32), lanes(q)]
        flight["x4", q] = (copy(line, line, dev(xx=xl)), right)

    def share(q):
        made = []
        for zz in (z, zl, zr):
            line = kv.at[zz, :, c, pl.ds(0, 32), lanes(q)]
            made.append(copy(line, line, dev(cc=other)))
        for xx in (x, xl, xr):
            line = kv.at[:, xx, c, pl.ds(32, 32), lanes(q)]
            made.append(copy(line, line, dev(cc=other)))
        flight["core", q] = made

    def share_far(q):
        for made in flight["z4", q] + flight["x4", q]:
            made.wait_recv()
        line = kv.at[(z + 2) % 4, :, c, pl.ds(0, 32), lanes(q)]
        flight["core", q].append(copy(line, line, dev(cc=other)))
        line = kv.at[:, (x + 2) % 4, c, pl.ds(32, 32), lanes(q)]
        flight["core", q].append(copy(line, line, dev(cc=other)))

    def score(q):
        for made in flight["q2", q]:
            made.wait_recv()
        for made in flight["core", q]:
            made.wait_recv()
        turned[...] = qb[:, :, lanes(q)].reshape(half, step).T

        @pl.loop(0, 8)
        def _(j):
            keys = kv[j // 2, pl.ds(j % 2 * 2, 2), :, :, lanes(q)].reshape(half, step)
            part = jnp.dot(keys, turned[...], preferred_element_type=F32)
            if q == 0:
                scores[j] = part
            else:
                scores[j] = scores[j] + part

    stages = ((fit, FIT), (pass_on, PASS), (begin, BEGIN), (relay, RELAY), (ask, ASK), (relay_ask, REASK), (widen, WIDEN),
              (relay_lines, LINES), (share, SHARE), (share_far, FAR), (score, SCORE))
    order = [(at[0] + at[1] * q, q, run) for run, at in stages for q in range(CHUNKS)]
    for _, q, run in sorted(order, key=lambda item: item[:2]):
        run(q)

    for made in weights:
        made.wait_recv()
    wsum[...] = jnp.sum(wbuf[...], axis=0)
    mine_occ = p // 2
    wrow = wsum[pl.ds(mine_occ, 1), :]

    from_virt = virt[:, pl.ds(pl.multiple_of(x % 2 * 512 + c * half, half), half)] - occ[mine_occ]
    key_e = jnp.broadcast_to(near[...], (8, half)).T[:, 0:1]
    for j in range(8):
        amp[j] = (scores[j] / (key_e + (from_virt - occ[j]))).T.astype(BF16)

    piece = naux // 8

    def gradient(at, slot):
        where = pl.ds(pl.multiple_of(at * piece, 128), piece)
        total = None
        for j in range(8):
            keys = kv[j // 2, pl.ds(j % 2 * 2, 2), :, :, where].reshape(half, piece)
            part = wrow[:, j:j + 1] * jnp.dot(amp[j], keys, preferred_element_type=F32)
            total = part if total is None else total + part
        gt[slot] = total

    far_made = []
    for cc in range(2):
        gradient((y + 2) % 4 * 2 + cc, cc)
        made = []
        for side, to in ((0, yl), (1, yr)):
            gs2[side, cc] = gt[cc, pl.ds(side * 128, 128), :].astype(BF16)
            made.append(copy(gs2.at[side, cc], gr2.at[side, cc], dev(yy=to)))
        far_made.append(made)
    base = counter[0]
    near_made = []
    for cc in range(2):
        for side, to in ((0, yl), (1, yr)):
            gradient(to * 2 + cc, side)
        for side, to in ((0, yl), (1, yr)):
            far_made[cc][side].wait_recv()
            add = pl.ds(side * 128, 128)
            gt[side, add, :] = gt[side, add, :] + gr2[side, cc].astype(F32)
            gs1[side, cc] = gt[side].astype(BF16)
            near_made.append(copy(gs1.at[side, cc], gr1.at[side, c], dev(yy=to, cc=cc), recv_at=base + side * 2 + c))
    gradient(y * 2 + other, 0)
    gp[...] = gt[0].astype(BF16)
    core_made = copy(gp, gpr, dev(cc=other))
    gradient(y * 2 + c, 1)

    for side in range(2):
        for core in range(2):
            pltpu.make_async_remote_copy(
                src_ref=gs1.at[side, core], dst_ref=gr1.at[side, core], send_sem=send.at[base],
                recv_sem=recv.at[base + side * 2 + core], device_id=dev(cc=other), device_id_type=MESH).wait_recv()
    core_made.wait_recv()
    mine = gt[1] + gr1[0, c].astype(F32) + gr1[1, c].astype(F32)
    out[:, mine_cols] = mine.T
    theirs = gpr[...].astype(F32) + gr1[0, other].astype(F32) + gr1[1, other].astype(F32)
    out[:, other_cols] = theirs.T
    for made in started:
        made.wait_send()
    assert counter[0] <= send.shape[0]


COPIES = 256


def on_device(integrals, metric, occ_energy, virt_energy, pair_table, pair_count):
    naux = metric.shape[1]
    y = lax.axis_index("aux") // 2
    near = lax.dynamic_index_in_dim(virt_energy.reshape(4, 4, 64), y, 1, keepdims=False).reshape(1, 256)
    vm = pl.BlockSpec(memory_space=pltpu.VMEM)
    sm = pl.BlockSpec(memory_space=pltpu.SMEM)
    V = pltpu.VMEM
    return pl.pallas_call(
        kernel,
        out_shape=jax.ShapeDtypeStruct((384, 512), F32),
        in_specs=[vm, pl.BlockSpec(memory_space=pl.ANY), vm, vm, sm, sm, sm],
        out_specs=vm,
        scratch_shapes=[
            V((4, 4, 2, 64, naux), BF16),
            V((4, 64, naux), BF16),
            V((16, 24, 512), BF16),
            V((16, 24, 256), BF16),
            V((2, 384, naux), BF16),
            V((256, 768), BF16),
            V((16, 8, 128), F32),
            V((8, 128), F32),
            V((256, naux), F32),
            V((2, 32, naux), I16), V((CHUNKS, 2, 8, 128), F32), V((2, 32, naux), I16), V((CHUNKS, 2, 8, 128), F32),
            V((2, 64, naux), I16), V((CHUNKS, 2, 8, 128), F32), V((2, 64, naux), I16), V((CHUNKS, 2, 8, 128), F32),
            V((naux // CHUNKS, 256), BF16),
            V((8, 256, 256), F32),
            V((8, 256, 256), BF16),
            V((2, 256, 384), F32),
            V((2, 2, 128, 384), BF16), V((2, 2, 128, 384), BF16),
            V((2, 2, 256, 384), BF16), V((2, 2, 256, 384), BF16),
            V((256, 384), BF16), V((256, 384), BF16),
            pltpu.SemaphoreType.DMA((COPIES,)),
            pltpu.SemaphoreType.DMA((COPIES,)),
            pltpu.SemaphoreType.DMA(()),
        ],
        compiler_params=pltpu.CompilerParams(
            collective_id=0, has_side_effects=True, vmem_limit_bytes=60 * 1024 * 1024),
    )(integrals, metric, virt_energy.reshape(1, -1), near, occ_energy, pair_table, pair_count)


def solution(mesh):
    placed = (P(("aux", "pair"), None), P("aux", None), P(), P(), P("pair", None), P("pair"))
    return jax.shard_map(
        on_device, mesh=mesh, in_specs=placed, out_specs=P("aux", "pair"), check_vma=False
    )
```
